128 devices in a mesh: row: 8 (over z, core), col: 16 (over y, x).
Axes of the slice: x: 4, y: 4, z: 4, core: 2. Of those that a mesh axis runs over, the one named last changes fastest.
Arguments:
- a_coupling: float32 [8192, 8192], P('row', 'col'), as said below
- rhs: float32 [8192, 8192], P('row', 'col'), as said below
- eig_vec: float32 [8192, 512], replicated, may hold values from -1 to 1, as said below
- eig_val: float32 [8192], replicated, may hold values from 0.5 to 2
Outputs:
- solution: float32 [8192, 8192], P('row', 'col')
- pending: float32 [8192, 8192], P('row', 'col')
The draws below stay inside these ranges and needn't reach their ends.
Inputs may be any that keep to these rules, and one draw needn't show every extreme that they name: `a_coupling`: in natural order A_ik is zero for k <= i: only tiles right of the diagonal tile carry values. `rhs`: symmetric. `eig_vec`: in natural order each block of 512 rows is an orthogonal matrix.
All inputs are finite; a program needn't handle non-finite values.
Results may differ from the reference program's by a relative error of at most 0.00011.
Values sent between devices are 32-bit elements; how exact they have to be, the bound alone decides.
No kernel may reach another device: no remote copies, remote signals or barrier semaphores. Data moves between devices by JAX's collectives and lax.ppermute only.
A program may use at most 192 MiB of HBM per device.

```python
import math
import jax
import jax.numpy as jnp
from jax import lax

TB = 512
TILES = 16
ORDER = 8192
WAVES = 8


def flip_trailing_drawn(natural):
    rest = natural.shape[1:]
    grouped = natural.reshape((2, TILES // 2, TB) + rest)
    return jnp.concatenate([grouped[:1], grouped[1:, ::-1]], axis=0).reshape(natural.shape)


def stored_rows_drawn(natural):
    rest = natural.shape[1:]
    flipped = flip_trailing_drawn(natural)
    return flipped.reshape((2, TILES, TB // 2) + rest).swapaxes(0, 1).reshape((ORDER,) + rest)


def draw_a_coupling(key, part):
    normal_draw = jax.random.normal(key, (ORDER, ORDER), jnp.float32) * (2.0 / ORDER ** 0.5)
    tile_ids = jnp.arange(ORDER) // TB
    upper = tile_ids[None, :] > tile_ids[:, None]
    natural = jnp.where(upper, normal_draw, 0.0)
    return stored_rows_drawn(stored_rows_drawn(natural).T).T.astype(jnp.float32)


def draw_rhs(key, part):
    normal_draw = jax.random.normal(jax.random.fold_in(key, 11), (ORDER, ORDER), jnp.float32)
    symmetric = (normal_draw + normal_draw.T) * 0.7071
    return symmetric.astype(jnp.float32)


def draw_eig_vec(key, part):
    normal_draw = jax.random.normal(jax.random.fold_in(key, 21), (TILES, TB, TB), jnp.float32)
    ortho, _ = jnp.linalg.qr(normal_draw)
    return stored_rows_drawn(ortho.reshape(ORDER, TB)).astype(jnp.float32)


def setup_inputs(seed: int = 0) -> dict:
    seeds = jax.random.split(jax.random.key(seed), 5)
    a_coupling = draw_a_coupling(jax.random.fold_in(seeds[4], 71), 0)
    rhs = draw_rhs(jax.random.fold_in(seeds[4], 71), 0)
    eig_vec = draw_eig_vec(jax.random.fold_in(seeds[4], 71), 0)
    eig_val = jnp.clip(jnp.exp(jax.random.uniform(seeds[3], (ORDER,), jnp.float32, math.log(0.5), math.log(2.0))), 0.5, 2.0)
    return dict(a_coupling=a_coupling, rhs=rhs, eig_vec=eig_vec, eig_val=eig_val)


def matmul(left_side, right_side):
    return jnp.dot(left_side.astype(jnp.float32), right_side.astype(jnp.float32), precision=lax.Precision.HIGHEST, preferred_element_type=jnp.float32)

def flip_trailing(natural):
    rest = natural.shape[1:]
    grouped = natural.reshape((2, TILES // 2, TB) + rest)
    return jnp.concatenate([grouped[:1], grouped[1:, ::-1]], axis=0).reshape(natural.shape)

def natural_rows(stored):
    rest = stored.shape[1:]
    plain = stored.reshape((TILES, 2, TB // 2) + rest).swapaxes(0, 1).reshape((ORDER,) + rest)
    return flip_trailing(plain)

def stored_rows(natural):
    rest = natural.shape[1:]
    flipped = flip_trailing(natural)
    return flipped.reshape((2, TILES, TB // 2) + rest).swapaxes(0, 1).reshape((ORDER,) + rest)

def natural_both(stored):
    return natural_rows(natural_rows(stored).T).T

def stored_both(natural):
    return stored_rows(stored_rows(natural).T).T

def reference(a_coupling, rhs, eig_vec, eig_val):
    a_natural = natural_both(a_coupling)
    rhs_natural = natural_both(rhs)
    vec_natural = natural_rows(eig_vec)
    val_natural = natural_rows(eig_val)
    tile_count = TILES
    solution = jnp.zeros_like(rhs_natural)
    pending = jnp.zeros_like(rhs_natural)
    for wave_step in range(WAVES):
        target = 2 * tile_count - 2 - wave_step
        solved = []
        for tile_row in range(tile_count):
            tile_col = target - tile_row
            if tile_col < 0 or tile_col >= tile_count:
                continue
            row_span = slice(tile_row * TB, (tile_row + 1) * TB)
            col_span = slice(tile_col * TB, (tile_col + 1) * TB)
            vec_row = vec_natural[row_span]
            vec_col = vec_natural[col_span]
            core_tile = matmul(matmul(vec_row.T, rhs_natural[row_span, col_span] - pending[row_span, col_span]), vec_col)
            divisor = -(val_natural[row_span][:, None] + val_natural[col_span][None, :])
            tile_value = matmul(matmul(vec_row, core_tile / divisor), vec_col.T)
            solution = solution.at[row_span, col_span].set(tile_value)
            solved.append((row_span, col_span, tile_value))
        for row_span, col_span, tile_value in solved:
            pending = pending.at[:, col_span].add(matmul(a_natural[:, row_span], tile_value))
            pending = pending.at[row_span, :].add(matmul(tile_value, a_natural[:, col_span].T))
    return (stored_both(solution), stored_both(pending))
```

```python
import functools

import jax
import jax.numpy as jnp
import numpy as np
from jax import lax
from jax.experimental import pallas as pl
from jax.experimental.pallas import tpu as pltpu
from jax.sharding import PartitionSpec as P


TB = 512
HB = 256
NT = 8


def mm(left_side, right_side, dims=None):
    if dims is None:
        dims = (((left_side.ndim - 1,), (0,)), ((), ()))
    return lax.dot_general(
        left_side, right_side, dims, precision=lax.Precision.HIGH, preferred_element_type=jnp.float32
    )


def tilewise(stored):
    quarter = stored.shape[0] // 4
    rest = stored.shape[1:]
    return stored.reshape((2, 2, quarter) + rest).swapaxes(0, 1).reshape(stored.shape)


def split(value):
    high = value.astype(jnp.bfloat16)
    low = (value - high.astype(jnp.float32)).astype(jnp.bfloat16)
    return high, low


def dot_nn(left, right):
    return lax.dot_general(left, right, (((1,), (0,)), ((), ())), preferred_element_type=jnp.float32)


def dot_nt(left, right):
    return lax.dot_general(left, right, (((1,), (1,)), ((), ())), preferred_element_type=jnp.float32)


def slot_of(p):
    return jnp.where(p >= 7, 25, jnp.where(p >= 6, 23, 4 * p))


def solve_kernel(
    rows_ref, cols_ref, a_ref, r_ref, val_row_ref, val_col_ref, out_ref,
    s_hi, s_lo, acc, t_hi, t_lo, stage, sems,
):
    step = pl.program_id(0)
    a = rows_ref[step]
    p = cols_ref[step]
    count = jnp.minimum(a, NT - a)

    def copies(a, b, i, j):
        return (
            pltpu.make_async_copy(
                stage.at[0], out_ref.at[pl.ds(a * TB, TB), pl.ds(b * TB, TB)], sems.at[0]
            ),
            pltpu.make_async_copy(
                stage.at[1], out_ref.at[pl.ds(i * TB, TB), pl.ds(j * TB, TB)], sems.at[1]
            ),
        )

    def residual(b, own):
        blocks = [
            [r_ref[b, 0, h, :, k * HB:(k + 1) * HB] for h in range(2)] for k in range(2)
        ]
        whole = jnp.concatenate([jnp.concatenate(row, axis=1) for row in blocks], axis=0)
        return whole - own

    def store(b, right_side, diagonal):
        tile = -(right_side / (val_col_ref[a] + val_row_ref[b]))
        high, low = split(tile)
        s_hi[slot_of(a) + b] = high
        s_lo[slot_of(a) + b] = low
        stage[0] = tile
        if diagonal:
            for copy in copies(a, b, NT - 1, NT - 1):
                copy.start()
        else:
            turned = tile.T
            stage[1] = turned

            @pl.when(a < 4)
            def _():
                high, low = split(turned)
                s_hi[4 * b + a] = high
                s_lo[4 * b + a] = low

            for copy in copies(a, b, b, a):
                copy.start()

    def drain():
        for copy in copies(0, 0, 0, 0):
            copy.wait()

    @pl.when(step == 0)
    def _():
        stage[1] = jnp.zeros_like(stage[1])
        store(0, residual(0, 0.0), True)

    @pl.when(step > 0)
    def _():
        slot = jnp.where(a < 4, step - 1, 6)
        for k in range(2):
            high, low = split(a_ref[0, 0, k])
            t_hi[slot, k * HB:(k + 1) * HB] = high
            t_lo[slot, k * HB:(k + 1) * HB] = low

        def product(b, carry):
            s = slot_of(p) + b
            value = dot_nn(t_hi[slot], s_hi[s])
            value += dot_nn(t_hi[slot], s_lo[s])
            value += dot_nn(t_lo[slot], s_hi[s])

            @pl.when(p == 0)
            def _():
                acc[b] = value

            @pl.when(p > 0)
            def _():
                acc[b] += value

            return carry

        lax.fori_loop(0, count, product, 0)

        def mirror(b, q, target):
            s = slot_of(a) + q
            t = b * (b - 1) // 2 + q
            value = dot_nt(s_hi[s], t_hi[t])
            value += dot_nt(s_hi[s], t_lo[t])
            value += dot_nt(s_lo[s], t_hi[t])
            acc[target] += value

        @pl.when(p == a - 1)
        def _():
            def tile(b, carry):
                def inner(q, carry):
                    mirror(b, q, b)
                    return carry

                lax.fori_loop(0, b, inner, 0)
                drain()
                store(b, residual(b, acc[b]), False)
                return carry

            lax.fori_loop(0, count, tile, 0)

            @pl.when(a < 4)
            def _():
                acc[0] = jnp.zeros_like(acc[0])

                def inner(q, carry):
                    mirror(a, q, 0)
                    return carry

                lax.fori_loop(0, a, inner, 0)
                drain()
                store(a, residual(a, acc[0] + acc[0].T), True)

    @pl.when(step == pl.num_programs(0) - 1)
    def _():
        drain()


def solve(gathered, values):
    pairs = [(1, 0)] + [(a, p) for a in range(1, NT) for p in range(a)]
    rows = np.array([0] + [a for a, _ in pairs[1:]], np.int32)
    cols = np.array([p for _, p in pairs], np.int32)
    grid_spec = pltpu.PrefetchScalarGridSpec(
        num_scalar_prefetch=2,
        grid=(len(pairs),),
        in_specs=[
            pl.BlockSpec(
                (1, 1, 2, HB, TB), lambda t, rows, cols: (jnp.maximum(rows[t], 1), cols[t], 0, 0, 0)
            ),
            pl.BlockSpec((4, 1, 2, HB, TB), lambda t, rows, cols: (0, rows[t], 0, 0, 0)),
            pl.BlockSpec((NT, 1, TB), lambda t, rows, cols: (0, 0, 0)),
            pl.BlockSpec((NT, TB, 1), lambda t, rows, cols: (0, 0, 0)),
        ],
        out_specs=pl.BlockSpec(memory_space=pl.ANY),
        scratch_shapes=[
            pltpu.VMEM((26, TB, TB), jnp.bfloat16),
            pltpu.VMEM((26, TB, TB), jnp.bfloat16),
            pltpu.VMEM((4, TB, TB), jnp.float32),
            pltpu.VMEM((7, TB, TB), jnp.bfloat16),
            pltpu.VMEM((7, TB, TB), jnp.bfloat16),
            pltpu.VMEM((2, TB, TB), jnp.float32),
            pltpu.SemaphoreType.DMA((2,)),
        ],
    )
    return pl.pallas_call(
        solve_kernel,
        grid_spec=grid_spec,
        out_shape=jax.ShapeDtypeStruct((NT * TB, NT * TB), jnp.float32),
        name="solve",
        cost_estimate=pl.CostEstimate(
            flops=84 * 6 * TB**3, bytes_accessed=90 * 2**20, transcendentals=0
        ),
        compiler_params=pltpu.CompilerParams(
            dimension_semantics=("arbitrary",), vmem_limit_bytes=63 * 2**20
        ),
    )(jnp.asarray(rows), jnp.asarray(cols), gathered, gathered,
      values.reshape(NT, 1, TB), values.reshape(NT, TB, 1))


def on_device(a_coupling, rhs, eig_vec, eig_val):
    row = lax.axis_index("row")
    col = lax.axis_index("col")
    half = col % 2
    tile_col = col // 2
    a_local = tilewise(a_coupling)
    lead = a_local[:TB, HB:]
    trail = a_local[TB:, HB:]
    rhs_trail = tilewise(rhs)[TB:, HB:]
    vectors = eig_vec.reshape(NT, 2, 2, HB, TB)[:, :, 1].reshape(NT, TB, TB)
    values = eig_val.reshape(NT, 2, 2, HB)[:, :, 1].reshape(NT, TB)
    vec_row = lax.dynamic_index_in_dim(vectors, row, 0, keepdims=False)
    vec_col = lax.dynamic_index_in_dim(vectors, tile_col, 0, keepdims=False)
    vec_half = lax.dynamic_slice_in_dim(vec_col, half * HB, HB, 0)

    coupled = tile_col < row
    left = mm(vec_row.T, jnp.where(coupled, trail, rhs_trail))
    kept = lax.dynamic_slice_in_dim(left, half * HB, HB, 0)
    sent = lax.dynamic_slice_in_dim(left, (1 - half) * HB, HB, 0)
    other = lax.ppermute(sent, "col", [(i, i ^ 1) for i in range(16)])
    both = jnp.where(
        half == 0, jnp.concatenate([kept, other], axis=1), jnp.concatenate([other, kept], axis=1)
    )
    part = mm(both, vec_col)
    turned = jnp.concatenate([part[:, :HB].T, part[:, HB:].T], axis=1)
    part = jnp.where(coupled, part, turned)
    gathered = lax.all_gather(part, ("row", "col"), axis=0, tiled=True)
    gathered = gathered.reshape(NT, NT, 2, HB, TB)

    lead_panel = lax.all_gather(lead, "col", axis=1, tiled=True)

    def place(r, c):
        return r * 16 + c

    pairs = [(r, c) for r in range(NT) for c in range(16)]
    straight = [(place(r, c), place(c // 2, 2 * r + c % 2)) for r, c in pairs]
    crossed = [(place(r, c), place(c // 2, 2 * r + 1 - c % 2)) for r, c in pairs]
    same = lax.ppermute(
        lax.dynamic_slice_in_dim(lead, half * HB, HB, 0), ("row", "col"), straight
    )
    cross = lax.ppermute(
        lax.dynamic_slice_in_dim(lead, (1 - half) * HB, HB, 0), ("row", "col"), crossed
    )
    block = jnp.where(
        half == 0, jnp.concatenate([same, cross], axis=1), jnp.concatenate([cross, same], axis=1)
    )
    ring = [block] + [
        lax.ppermute(block, "row", [(i, (i + 2 * d) % NT) for i in range(NT)]) for d in (1, 2, 3)
    ]
    mine = jnp.stack(ring)
    theirs = lax.ppermute(mine, "row", [(i, i ^ 1) for i in range(NT)])
    core = row % 2
    z = row // 2
    stacked = jnp.stack([jnp.where(core == 0, mine, theirs), jnp.where(core == 0, theirs, mine)], 1)
    order = (z - jnp.arange(4)) % 4
    col_panel = stacked[order].reshape(NT, HB, TB)
    col_panel = mm(col_panel, vectors, (((2,), (1,)), ((0,), (0,))))

    solved = solve(gathered, values)

    tiles = jnp.arange(NT)
    a_row = lax.dynamic_index_in_dim(gathered, row, 0, keepdims=False).reshape(NT, TB, TB)
    a_row = jnp.where((tiles < row)[:, None, None], a_row, 0)
    a_col = lax.dynamic_index_in_dim(gathered, tile_col, 0, keepdims=False).reshape(NT, TB, TB)
    a_col = jnp.where((tiles < tile_col)[:, None, None], a_col, 0)
    mirror = mm(a_col, vec_half, (((1,), (1,)), ((), ())))

    s_col = lax.dynamic_slice_in_dim(solved, tile_col * TB, TB, 1).reshape(NT, TB, TB)
    s_col = jnp.where((tiles + tile_col < NT)[:, None, None], s_col, 0)
    half_turned = mm(s_col, vec_half, (((2,), (1,)), ((), ())))
    x_col = mm(vectors, half_turned, (((2,), (1,)), ((0,), (0,))))
    pending_lead = mm(lead_panel, x_col.reshape(NT * TB, HB))
    trail_sum = mm(a_row, half_turned, (((2,), (1,)), ((0,), (0,)))).sum(0)

    s_row = lax.dynamic_slice_in_dim(solved, row * TB, TB, 0)
    s_row = jnp.where((jnp.arange(NT * TB) // TB + row < NT)[None, :], s_row, 0)
    right_side = jnp.concatenate([col_panel.swapaxes(1, 2), mirror], axis=2).reshape(NT * TB, TB)
    row_sum = mm(s_row, right_side)
    row_sum = row_sum + jnp.concatenate([jnp.zeros_like(trail_sum), trail_sum], axis=1)
    pending_trail = mm(vec_row, row_sum)

    x_own = lax.dynamic_index_in_dim(x_col, row, 0, keepdims=False)
    x_own = jnp.where(row + tile_col < NT, x_own, 0)
    zero = jnp.zeros((TB, HB), jnp.float32)
    solution = jnp.concatenate(
        [jnp.zeros((TB, TB), jnp.float32), jnp.concatenate([zero, x_own], axis=1)], axis=0
    )
    pending = jnp.concatenate(
        [jnp.concatenate([zero, pending_lead], axis=1), pending_trail], axis=0
    )
    return (tilewise(solution), tilewise(pending))


def solution(mesh):
    return jax.shard_map(
        on_device,
        mesh=mesh,
        in_specs=(P("row", "col"), P("row", "col"), P(), P()),
        out_specs=(P("row", "col"), P("row", "col")),
        check_vma=False,
    )
```

```python
import functools

import jax
import jax.numpy as jnp
import numpy as np
from jax import lax
from jax.experimental import pallas as pl
from jax.experimental.layout import Layout, with_layout_constraint
from jax.experimental.pallas import tpu as pltpu
from jax.sharding import PartitionSpec as P


TB = 512
HB = 256
NT = 8


def mm(left_side, right_side, dims=None):
    if dims is None:
        dims = (((left_side.ndim - 1,), (0,)), ((), ()))
    return lax.dot_general(
        left_side, right_side, dims, precision=lax.Precision.HIGH, preferred_element_type=jnp.float32
    )


def plain(value):
    return with_layout_constraint(value, Layout((0, 1)))


def split(value):
    high = value.astype(jnp.bfloat16)
    low = (value - high.astype(jnp.float32)).astype(jnp.bfloat16)
    return high, low


def dot_nn(left, right):
    return lax.dot_general(left, right, (((1,), (0,)), ((), ())), preferred_element_type=jnp.float32)


def dot_nt(left, right):
    return lax.dot_general(left, right, (((1,), (1,)), ((), ())), preferred_element_type=jnp.float32)


def slot_of(p):
    return jnp.where(p >= 7, 25, jnp.where(p >= 6, 23, 4 * p))


def solve_kernel(
    rows_ref, cols_ref, a_ref, r_ref, val_row_ref, val_col_ref, out_ref,
    s_hi, s_lo, acc, t_hi, t_lo, stage, sems,
):
    step = pl.program_id(0)
    a = rows_ref[step]
    p = cols_ref[step]
    count = jnp.minimum(a, NT - a)

    def copies(a, b, i, j):
        return (
            pltpu.make_async_copy(
                stage.at[0], out_ref.at[pl.ds(a * TB, TB), pl.ds(b * TB, TB)], sems.at[0]
            ),
            pltpu.make_async_copy(
                stage.at[1], out_ref.at[pl.ds(i * TB, TB), pl.ds(j * TB, TB)], sems.at[1]
            ),
        )

    def residual(b, own):
        blocks = [
            [r_ref[b, 0, h, :, k * HB:(k + 1) * HB] for h in range(2)] for k in range(2)
        ]
        whole = jnp.concatenate([jnp.concatenate(row, axis=1) for row in blocks], axis=0)
        return whole + own

    def store(b, right_side, diagonal):
        tile = -(right_side / (val_col_ref[a] + val_row_ref[b]))
        high, low = split(tile)
        s_hi[slot_of(a) + b] = high
        s_lo[slot_of(a) + b] = low
        stage[0] = tile
        if diagonal:
            for copy in copies(a, b, NT - 1, NT - 1):
                copy.start()
        else:
            turned = tile.T
            stage[1] = turned

            @pl.when(a < 4)
            def _():
                high, low = split(turned)
                s_hi[4 * b + a] = high
                s_lo[4 * b + a] = low

            for copy in copies(a, b, b, a):
                copy.start()

    def drain():
        for copy in copies(0, 0, 0, 0):
            copy.wait()

    @pl.when(step == 0)
    def _():
        stage[1] = jnp.zeros_like(stage[1])
        store(0, residual(0, 0.0), True)

    @pl.when(step > 0)
    def _():
        slot = jnp.where(a < 4, step - 1, 6)
        for k in range(2):
            high, low = split(a_ref[0, 0, k])
            t_hi[slot, k * HB:(k + 1) * HB] = high
            t_lo[slot, k * HB:(k + 1) * HB] = low

        @pl.when(p == 0)
        def _():
            def begin(b, carry):
                for k in range(2):
                    for h in range(2):
                        acc[b, k * HB:(k + 1) * HB, h * HB:(h + 1) * HB] = r_ref[
                            b, 0, h, :, k * HB:(k + 1) * HB
                        ]
                return carry

            lax.fori_loop(0, count, begin, 0)

        def product(b, carry):
            s = slot_of(p) + b
            high, low = t_hi[slot], t_lo[slot]
            right_high, right_low = s_hi[s], s_lo[s]
            acc[b] -= dot_nn(high, right_high) + dot_nn(high, right_low) + dot_nn(low, right_high)
            return carry

        lax.fori_loop(0, count, product, 0)

        def mirror(b, q, target):
            s = slot_of(a) + q
            t = b * (b - 1) // 2 + q
            high, low = s_hi[s], s_lo[s]
            right_high, right_low = t_hi[t], t_lo[t]
            acc[target] -= dot_nt(high, right_high) + dot_nt(high, right_low) + dot_nt(low, right_high)

        @pl.when(p == a - 1)
        def _():
            def tile(b, carry):
                def inner(q, carry):
                    mirror(b, q, b)
                    return carry

                lax.fori_loop(0, b, inner, 0)
                drain()
                store(b, acc[b], False)
                return carry

            lax.fori_loop(0, count, tile, 0)

            @pl.when(a < 4)
            def _():
                acc[0] = jnp.zeros_like(acc[0])

                def inner(q, carry):
                    mirror(a, q, 0)
                    return carry

                lax.fori_loop(0, a, inner, 0)
                drain()
                store(a, residual(a, acc[0] + acc[0].T), True)

    @pl.when(step == pl.num_programs(0) - 1)
    def _():
        drain()


def solve(gathered, val_row, val_col):
    pairs = [(1, 0)] + [(a, p) for a in range(1, NT) for p in range(a)]
    rows = np.array([0] + [a for a, _ in pairs[1:]], np.int32)
    cols = np.array([p for _, p in pairs], np.int32)
    grid_spec = pltpu.PrefetchScalarGridSpec(
        num_scalar_prefetch=2,
        grid=(len(pairs),),
        in_specs=[
            pl.BlockSpec(
                (1, 1, 2, HB, TB), lambda t, rows, cols: (jnp.maximum(rows[t], 1), cols[t], 0, 0, 0)
            ),
            pl.BlockSpec((4, 1, 2, HB, TB), lambda t, rows, cols: (0, rows[t], 0, 0, 0)),
            pl.BlockSpec((NT, 1, TB), lambda t, rows, cols: (0, 0, 0)),
            pl.BlockSpec((NT, TB, 1), lambda t, rows, cols: (0, 0, 0)),
        ],
        out_specs=pl.BlockSpec(memory_space=pl.ANY),
        scratch_shapes=[
            pltpu.VMEM((26, TB, TB), jnp.bfloat16),
            pltpu.VMEM((26, TB, TB), jnp.bfloat16),
            pltpu.VMEM((4, TB, TB), jnp.float32),
            pltpu.VMEM((7, TB, TB), jnp.bfloat16),
            pltpu.VMEM((7, TB, TB), jnp.bfloat16),
            pltpu.VMEM((2, TB, TB), jnp.float32),
            pltpu.SemaphoreType.DMA((2,)),
        ],
    )
    return pl.pallas_call(
        solve_kernel,
        grid_spec=grid_spec,
        out_shape=jax.ShapeDtypeStruct((NT * TB, NT * TB), jnp.float32),
        name="solve",
        cost_estimate=pl.CostEstimate(
            flops=84 * 6 * TB**3, bytes_accessed=90 * 2**20, transcendentals=0
        ),
        compiler_params=pltpu.CompilerParams(
            dimension_semantics=("arbitrary",), vmem_limit_bytes=63 * 2**20
        ),
    )(jnp.asarray(rows), jnp.asarray(cols), gathered, gathered, val_row, val_col)


def dot3(left, right, dot):
    left_high, left_low = left
    right_high, right_low = right
    return dot(left_high, right_high) + (dot(left_high, right_low) + dot(left_low, right_high))


def final_kernel(
    place_ref, s_col_ref, s_row_ref, v_p_ref, v_row_ref, v_half_ref, lead_ref, panel_ref,
    a_row_ref, a_col_ref, solution_ref, pending_ref, lead_sum, trail_sum, turn_sum, mirror_sum,
):
    p = pl.program_id(0)
    a = place_ref[0]
    b = place_ref[1]

    def whole(ref, i):
        return split(jnp.concatenate([ref[i(0)], ref[i(1)]], axis=0))

    v_half = split(v_half_ref[0, 0, 0])

    @pl.when(p == 0)
    def _():
        for ref in (lead_sum, trail_sum, turn_sum, mirror_sum, solution_ref):
            ref[...] = jnp.zeros_like(ref)

    v_p = whole(v_p_ref, lambda k: (0, k, 0))
    s_col = split(jnp.where(p + b < NT, s_col_ref[...], 0.0))
    s_row = split(jnp.where(p + a < NT, s_row_ref[...], 0.0))
    turned = dot3(s_col, v_half, dot_nt)
    panel = dot3(split(panel_ref[0]), v_p, dot_nn)
    turned = split(turned)
    x = dot3(v_p, turned, dot_nn)
    turn_sum[...] += dot3(s_row, split(panel), dot_nt)
    lead = split(jnp.concatenate([lead_ref[0, 0], lead_ref[0, 1]], axis=1))
    lead_sum[...] += dot3(lead, split(x), dot_nn)

    @pl.when((p < a) & (p + b < NT))
    def _():
        trail_sum[...] += dot3(whole(a_row_ref, lambda k: (0, 0, k)), turned, dot_nn)

    @pl.when((p == a) & (p + b < NT))
    def _():
        solution_ref[HB:2 * HB, HB:] = x[:HB]
        solution_ref[3 * HB:, HB:] = x[HB:]

    @pl.when((p < b) & (p + a < NT))
    def _():
        mirror_sum[...] += dot3(s_row, whole(a_col_ref, lambda k: (0, 0, k)), dot_nt)

    @pl.when(p == NT - 1)
    def _():
        v_row = whole(v_row_ref, lambda k: (0, k, 0))
        trail = trail_sum[...] + dot3(split(mirror_sum[...]), v_half, dot_nt)
        turn = dot3(v_row, split(turn_sum[...]), dot_nn)
        trail = dot3(v_row, split(trail), dot_nn)
        for k in range(2):
            own = slice(k * HB, (k + 1) * HB)
            top = slice(2 * k * HB, (2 * k + 1) * HB)
            low = slice((2 * k + 1) * HB, (2 * k + 2) * HB)
            pending_ref[top, :HB] = jnp.zeros((HB, HB), jnp.float32)
            pending_ref[top, HB:] = lead_sum[own]
            pending_ref[low, :HB] = turn[own]
            pending_ref[low, HB:] = trail[own]


def finish(place, solved, vectors, lead, panel, gathered):
    tile = (1, 1, 2, HB, TB)
    least = jnp.minimum

    def coupled_block(p, own, across):
        return (own, least(p, jnp.maximum(least(own - 1, NT - 1 - across), 0)), 0, 0, 0)

    grid_spec = pltpu.PrefetchScalarGridSpec(
        num_scalar_prefetch=1,
        grid=(NT,),
        in_specs=[
            pl.BlockSpec((TB, TB), lambda p, at: (least(p, NT - 1 - at[1]), at[1])),
            pl.BlockSpec((TB, TB), lambda p, at: (at[0], least(p, NT - 1 - at[0]))),
            pl.BlockSpec((1, 2, 1, HB, TB), lambda p, at: (p, 0, 1, 0, 0)),
            pl.BlockSpec((1, 2, 1, HB, TB), lambda p, at: (at[0], 0, 1, 0, 0)),
            pl.BlockSpec((1, 1, 1, HB, TB), lambda p, at: (at[1], at[2], 1, 0, 0)),
            pl.BlockSpec((1, 2, TB, HB), lambda p, at: (least(p, NT - 1 - at[1]), 0, 0, 0)),
            pl.BlockSpec((1, HB, TB), lambda p, at: (least(p, NT - 1 - at[0]), 0, 0)),
            pl.BlockSpec(tile, lambda p, at: coupled_block(p, at[0], at[1])),
            pl.BlockSpec(tile, lambda p, at: coupled_block(p, at[1], at[0])),
        ],
        out_specs=[pl.BlockSpec((2 * TB, TB), lambda p, at: (0, 0))] * 2,
        scratch_shapes=[pltpu.VMEM((TB, HB), jnp.float32)] * 3 + [pltpu.VMEM((TB, TB), jnp.float32)],
    )
    return pl.pallas_call(
        final_kernel,
        grid_spec=grid_spec,
        out_shape=[jax.ShapeDtypeStruct((2 * TB, TB), jnp.float32)] * 2,
        name="finish",
        cost_estimate=pl.CostEstimate(
            flops=25 * 6 * TB**3, bytes_accessed=64 * 2**20, transcendentals=0
        ),
        compiler_params=pltpu.CompilerParams(
            dimension_semantics=("arbitrary",), vmem_limit_bytes=60 * 2**20
        ),
    )(place, solved, solved, vectors, vectors, vectors, lead, panel, gathered, gathered)


def on_device(a_coupling, rhs, eig_vec, eig_val):
    row = lax.axis_index("row")
    col = lax.axis_index("col")
    half = col % 2
    tile_col = col // 2

    def trailing(stored):
        return jnp.concatenate([stored[HB:2 * HB, HB:], stored[3 * HB:, HB:]], axis=0)

    lead = plain(jnp.concatenate([a_coupling[:HB, HB:], a_coupling[2 * HB:3 * HB, HB:]], axis=0))
    vectors = eig_vec.reshape(NT, 2, 2, HB, TB)
    values = eig_val.reshape(NT, 2, 2, HB)[:, :, 1].reshape(NT, TB)

    def tile_vectors(index):
        return lax.dynamic_slice(
            vectors, (index, 0, 1, 0, 0), (1, 2, 1, HB, TB)
        ).reshape(TB, TB)

    coupled = tile_col < row
    left = mm(tile_vectors(row).T, jnp.where(coupled, trailing(a_coupling), trailing(rhs)))
    kept = lax.dynamic_slice_in_dim(left, half * HB, HB, 0)
    sent = lax.dynamic_slice_in_dim(left, (1 - half) * HB, HB, 0)
    other = lax.ppermute(sent, "col", [(i, i ^ 1) for i in range(16)])
    both = jnp.where(
        half == 0, jnp.concatenate([kept, other], axis=1), jnp.concatenate([other, kept], axis=1)
    )
    part = mm(both, tile_vectors(tile_col))
    turned = jnp.concatenate([part[:, :HB].T, part[:, HB:].T], axis=1)
    part = jnp.where(coupled, part, turned)
    gathered = lax.all_gather(part, ("row", "col"), axis=0, tiled=True)

    def place(r, c):
        return r * 16 + c

    held, _ = lax.optimization_barrier((lead, other))
    pairs = [(r, c) for r in range(NT) for c in range(16)]
    straight = [(place(r, c), place(c // 2, 2 * r + c % 2)) for r, c in pairs]
    crossed = [(place(r, c), place(c // 2, 2 * r + 1 - c % 2)) for r, c in pairs]
    same = lax.ppermute(
        plain(lax.dynamic_slice_in_dim(held, half * HB, HB, 0)), ("row", "col"), straight
    )
    cross = lax.ppermute(
        plain(lax.dynamic_slice_in_dim(held, (1 - half) * HB, HB, 0)), ("row", "col"), crossed
    )
    block = plain(jnp.where(
        half == 0, jnp.concatenate([same, cross], axis=1), jnp.concatenate([cross, same], axis=1)
    ))
    val_row = values.reshape(NT, 1, TB)
    val_col = values.reshape(NT, TB, 1)
    lead, block, gathered, val_row, val_col = lax.optimization_barrier(
        (lead, block, gathered, val_row, val_col)
    )
    gathered = gathered.reshape(NT, NT, 2, HB, TB)

    lead_panel = lax.all_gather(plain(lead), "col", axis=0, tiled=True).reshape(NT, 2, TB, HB)
    col_panel = lax.all_gather(plain(block), "row", axis=0, tiled=True).reshape(NT, HB, TB)

    solved = solve(gathered, val_row, val_col)
    position = jnp.stack([row, tile_col, half]).astype(jnp.int32)
    return tuple(finish(position, solved, vectors, lead_panel, col_panel, gathered))


def solution(mesh):
    return jax.shard_map(
        on_device,
        mesh=mesh,
        in_specs=(P("row", "col"), P("row", "col"), P(), P()),
        out_specs=(P("row", "col"), P("row", "col")),
        check_vma=False,
    )
```

```python
import functools

import jax
import jax.numpy as jnp
import numpy as np
from jax import lax
from jax.experimental import pallas as pl
from jax.experimental.layout import Layout, with_layout_constraint
from jax.experimental.pallas import tpu as pltpu
from jax.sharding import PartitionSpec as P


TB = 512
HB = 256
NT = 8
QB = 64
MB = HB - QB


def spread_pairs():
    pairs = [(i, j) for i in range(NT) for j in range(NT)]
    idle = [(i, j) for i, j in pairs if i <= j and i + j >= NT]
    active = [pair for pair in pairs if pair not in idle]

    def ring(left, right):
        return min((left - right) % 4, (right - left) % 4)

    def distance(left, right):
        return (
            ring(left[0] // 2, right[0] // 2) + ring(left[1] // 2, right[1] // 2)
            + 2 * (left[1] % 2 != right[1] % 2)
        )

    found = {}
    for slot in range(3):
        for home in idle:
            near = min((p for p in active if p not in found), key=lambda p: distance(p, home))
            found[near] = (home[0], home[1], slot)
    return found


SPREAD = spread_pairs()
TABLE = np.array(
    [SPREAD.get((i, j), (0, 0, 0)) for i in range(NT) for j in range(NT)], np.int32
).reshape(-1)
EXTRA = (1, 1, 2, 1, QB, TB)


def extra_block(table, i, j):
    at = 3 * (NT * (i % NT) + j % NT)
    return (table[at], table[at + 1], 0, table[at + 2], 0, 0)


def mm(left_side, right_side, dims=None):
    if dims is None:
        dims = (((left_side.ndim - 1,), (0,)), ((), ()))
    return lax.dot_general(
        left_side, right_side, dims, precision=lax.Precision.HIGH, preferred_element_type=jnp.float32
    )


def plain(value):
    return with_layout_constraint(value, Layout((0, 1)))


def split(value):
    high = value.astype(jnp.bfloat16)
    low = (value - high.astype(jnp.float32)).astype(jnp.bfloat16)
    return high, low


def dot_nn(left, right):
    return lax.dot_general(left, right, (((1,), (0,)), ((), ())), preferred_element_type=jnp.float32)


def dot_nt(left, right):
    return lax.dot_general(left, right, (((1,), (1,)), ((), ())), preferred_element_type=jnp.float32)


def slot_of(p):
    return jnp.where(p >= 7, 25, jnp.where(p >= 6, 23, 4 * p))


def solve_kernel(
    rows_ref, cols_ref, table_ref, a_ref, a_extra_ref, r_ref, r_extra_0, r_extra_1, r_extra_2,
    r_extra_3, val_row_ref, val_col_ref, out_ref, s_hi, s_lo, acc, t_hi, t_lo, stage, sems,
):
    step = pl.program_id(0)
    a = rows_ref[step]
    p = cols_ref[step]
    count = jnp.minimum(a, NT - a)

    def copies(n, a, b, i, j):
        return (
            pltpu.make_async_copy(
                stage.at[2 * n], out_ref.at[pl.ds(a * TB, TB), pl.ds(b * TB, TB)], sems.at[2 * n]
            ),
            pltpu.make_async_copy(
                stage.at[2 * n + 1], out_ref.at[pl.ds(i * TB, TB), pl.ds(j * TB, TB)],
                sems.at[2 * n + 1],
            ),
        )

    def drain(n):
        for copy in copies(n, 0, 0, 0, 0):
            copy.wait()

    for b, extra in enumerate((r_extra_0, r_extra_1, r_extra_2, r_extra_3)):
        @pl.when((p == 0) & ((b < count) | (b == a)))
        def _():
            for k in range(2):
                for h in range(2):
                    own = slice(k * HB, (k + 1) * HB)
                    across = slice(h * HB, (h + 1) * HB)
                    acc[b, k * HB:k * HB + MB, across] = r_ref[b, 0, h, :, own]
                    acc[b, k * HB + MB:(k + 1) * HB, across] = extra[0, 0, h, 0, :, own]

    def store(b, right_side, diagonal):
        tile = -(right_side / (val_col_ref[a] + val_row_ref[b]))
        high, low = split(tile)
        s_hi[slot_of(a) + b] = high
        s_lo[slot_of(a) + b] = low
        n = b % 2
        stage[2 * n] = tile
        if diagonal:
            for copy in copies(n, a, b, NT - 1, NT - 1):
                copy.start()
        else:
            turned = tile.T
            stage[2 * n + 1] = turned

            @pl.when(a < 4)
            def _():
                high, low = split(turned)
                s_hi[4 * b + a] = high
                s_lo[4 * b + a] = low

            for copy in copies(n, a, b, b, a):
                copy.start()

    @pl.when(step == 0)
    def _():
        stage[1] = jnp.zeros_like(stage[1])
        stage[3] = jnp.zeros_like(stage[3])
        store(0, acc[0], True)

    @pl.when(step > 0)
    def _():
        slot = jnp.where(a < 4, step - 1, 6)
        for k in range(2):
            high, low = split(a_ref[0, 0, k])
            t_hi[slot, k * HB:k * HB + MB] = high
            t_lo[slot, k * HB:k * HB + MB] = low
            high, low = split(a_extra_ref[0, 0, k, 0])
            t_hi[slot, k * HB + MB:(k + 1) * HB] = high
            t_lo[slot, k * HB + MB:(k + 1) * HB] = low

        def product(b, carry):
            s = slot_of(p) + b
            high, low = t_hi[slot], t_lo[slot]
            right_high, right_low = s_hi[s], s_lo[s]
            acc[b] -= dot_nn(high, right_high) + dot_nn(high, right_low) + dot_nn(low, right_high)
            return carry

        lax.fori_loop(0, count, product, 0)

        def mirror(b, q, target):
            s = slot_of(a) + q
            t = b * (b - 1) // 2 + q
            high, low = s_hi[s], s_lo[s]
            right_high, right_low = t_hi[t], t_lo[t]
            acc[target] -= dot_nt(high, right_high) + dot_nt(high, right_low) + dot_nt(low, right_high)

        @pl.when(p == a - 1)
        def _():
            def tile(b, carry):
                def inner(q, carry):
                    mirror(b, q, b)
                    return carry

                lax.fori_loop(0, b, inner, 0)
                drain(b % 2)
                store(b, acc[b], False)
                return carry

            lax.fori_loop(0, count, tile, 0)

            @pl.when(a < 4)
            def _():
                acc[0] = jnp.zeros_like(acc[0])

                def inner(q, carry):
                    mirror(a, q, 0)
                    return carry

                lax.fori_loop(0, a, inner, 0)

                @pl.when(a > 1)
                def _():
                    drain(a % 2)

                store(a, acc[a] + acc[0] + acc[0].T, True)

    @pl.when(step == pl.num_programs(0) - 1)
    def _():
        drain(0)
        drain(1)


def solve(gathered, val_row, val_col):
    pairs = [(1, 0)] + [(a, p) for a in range(1, NT) for p in range(a)]
    extras = gathered.reshape(NT, NT, 2, 3, QB, TB)
    def at(t):
        return jnp.clip(t, 0, len(pairs) - 1)

    rows = np.array([0] + [a for a, _ in pairs[1:]] + [0] * 3, np.int32)
    cols = np.array([p for _, p in pairs] + [0] * 3, np.int32)
    grid_spec = pltpu.PrefetchScalarGridSpec(
        num_scalar_prefetch=3,
        grid=(len(pairs),),
        in_specs=[
            pl.BlockSpec(
                (1, 1, 2, MB, TB),
                lambda t, rows, cols, table: (jnp.maximum(rows[at(t)], 1), cols[at(t)], 0, 0, 0),
            ),
            pl.BlockSpec(
                EXTRA,
                lambda t, rows, cols, table: extra_block(
                    table, jnp.maximum(rows[at(t)], 1), cols[at(t)]
                ),
            ),
            pl.BlockSpec((4, 1, 2, MB, TB), lambda t, rows, cols, table: (0, rows[at(t)], 0, 0, 0)),
        ] + [
            pl.BlockSpec(
                EXTRA,
                functools.partial(
                    lambda b, t, rows, cols, table: extra_block(table, b, rows[at(t)]), b
                ),
            )
            for b in range(4)
        ] + [
            pl.BlockSpec((NT, 1, TB), lambda t, rows, cols, table: (0, 0, 0)),
            pl.BlockSpec((NT, TB, 1), lambda t, rows, cols, table: (0, 0, 0)),
        ],
        out_specs=pl.BlockSpec(memory_space=pl.ANY),
        scratch_shapes=[
            pltpu.VMEM((26, TB, TB), jnp.bfloat16),
            pltpu.VMEM((26, TB, TB), jnp.bfloat16),
            pltpu.VMEM((4, TB, TB), jnp.float32),
            pltpu.VMEM((7, TB, TB), jnp.bfloat16),
            pltpu.VMEM((7, TB, TB), jnp.bfloat16),
            pltpu.VMEM((4, TB, TB), jnp.float32),
            pltpu.SemaphoreType.DMA((4,)),
        ],
    )
    return pl.pallas_call(
        solve_kernel,
        grid_spec=grid_spec,
        out_shape=jax.ShapeDtypeStruct((NT * TB, NT * TB), jnp.float32),
        name="solve",
        cost_estimate=pl.CostEstimate(
            flops=84 * 6 * TB**3, bytes_accessed=90 * 2**20, transcendentals=0
        ),
        compiler_params=pltpu.CompilerParams(
            dimension_semantics=("arbitrary",), vmem_limit_bytes=63 * 2**20
        ),
    )(
        jnp.asarray(rows), jnp.asarray(cols), jnp.asarray(TABLE), gathered, extras, gathered,
        extras, extras, extras, extras, val_row, val_col,
    )


def dot3(left, right, dot):
    left_high, left_low = left
    right_high, right_low = right
    return dot(left_high, right_high) + (dot(left_high, right_low) + dot(left_low, right_high))


def final_kernel(
    place_ref, table_ref, s_col_ref, s_row_ref, v_p_ref, v_row_ref, v_half_ref, lead_ref, panel_ref,
    a_row_ref, a_row_extra_ref, a_col_ref, a_col_extra_ref, solution_ref, pending_ref, lead_sum, trail_sum, turn_sum, mirror_sum,
):
    p = pl.program_id(0)
    a = place_ref[0]
    b = place_ref[1]

    def whole(ref, i):
        return split(jnp.concatenate([ref[i(0)], ref[i(1)]], axis=0))

    def joined(ref, extra):
        parts = [ref[0, 0, 0], extra[0, 0, 0, 0], ref[0, 0, 1], extra[0, 0, 1, 0]]
        return split(jnp.concatenate(parts, axis=0))

    v_half = split(v_half_ref[0, 0, 0])

    @pl.when(p == 0)
    def _():
        for ref in (lead_sum, trail_sum, turn_sum, mirror_sum, solution_ref):
            ref[...] = jnp.zeros_like(ref)

    v_p = whole(v_p_ref, lambda k: (0, k, 0))
    s_col = split(jnp.where(p + b < NT, s_col_ref[...], 0.0))
    s_row = split(jnp.where(p + a < NT, s_row_ref[...], 0.0))
    turned = dot3(s_col, v_half, dot_nt)
    panel = dot3(split(panel_ref[0]), v_p, dot_nn)
    turned = split(turned)
    x = dot3(v_p, turned, dot_nn)
    turn_sum[...] += dot3(s_row, split(panel), dot_nt)
    lead = split(jnp.concatenate([lead_ref[0, 0], lead_ref[0, 1]], axis=1))
    lead_sum[...] += dot3(lead, split(x), dot_nn)

    @pl.when((p < a) & (p + b < NT))
    def _():
        trail_sum[...] += dot3(joined(a_row_ref, a_row_extra_ref), turned, dot_nn)

    @pl.when((p == a) & (p + b < NT))
    def _():
        solution_ref[HB:2 * HB, HB:] = x[:HB]
        solution_ref[3 * HB:, HB:] = x[HB:]

    @pl.when((p < b) & (p + a < NT))
    def _():
        mirror_sum[...] += dot3(s_row, joined(a_col_ref, a_col_extra_ref), dot_nt)

    @pl.when(p == NT - 1)
    def _():
        v_row = whole(v_row_ref, lambda k: (0, k, 0))
        trail = trail_sum[...] + dot3(split(mirror_sum[...]), v_half, dot_nt)
        turn = dot3(v_row, split(turn_sum[...]), dot_nn)
        trail = dot3(v_row, split(trail), dot_nn)
        for k in range(2):
            own = slice(k * HB, (k + 1) * HB)
            top = slice(2 * k * HB, (2 * k + 1) * HB)
            low = slice((2 * k + 1) * HB, (2 * k + 2) * HB)
            pending_ref[top, :HB] = jnp.zeros((HB, HB), jnp.float32)
            pending_ref[top, HB:] = lead_sum[own]
            pending_ref[low, :HB] = turn[own]
            pending_ref[low, HB:] = trail[own]


def finish(place, solved, vectors, lead, panel, gathered):
    tile = (1, 1, 2, MB, TB)
    least = jnp.minimum

    def coupled_block(p, own, across):
        return (own, least(p, jnp.maximum(least(own - 1, NT - 1 - across), 0)), 0, 0, 0)

    def coupled_extra(table, p, own, across):
        return extra_block(table, *coupled_block(p, own, across)[:2])

    extras = gathered.reshape(NT, NT, 2, 3, QB, TB)
    grid_spec = pltpu.PrefetchScalarGridSpec(
        num_scalar_prefetch=2,
        grid=(NT,),
        in_specs=[
            pl.BlockSpec((TB, TB), lambda p, at, table: (least(p, NT - 1 - at[1]), at[1])),
            pl.BlockSpec((TB, TB), lambda p, at, table: (at[0], least(p, NT - 1 - at[0]))),
            pl.BlockSpec((1, 2, 1, HB, TB), lambda p, at, table: (p, 0, 1, 0, 0)),
            pl.BlockSpec((1, 2, 1, HB, TB), lambda p, at, table: (at[0], 0, 1, 0, 0)),
            pl.BlockSpec((1, 1, 1, HB, TB), lambda p, at, table: (at[1], at[2], 1, 0, 0)),
            pl.BlockSpec((1, 2, TB, HB), lambda p, at, table: (least(p, NT - 1 - at[1]), 0, 0, 0)),
            pl.BlockSpec((1, HB, TB), lambda p, at, table: (least(p, NT - 1 - at[0]), 0, 0)),
            pl.BlockSpec(tile, lambda p, at, table: coupled_block(p, at[0], at[1])),
            pl.BlockSpec(EXTRA, lambda p, at, table: coupled_extra(table, p, at[0], at[1])),
            pl.BlockSpec(tile, lambda p, at, table: coupled_block(p, at[1], at[0])),
            pl.BlockSpec(EXTRA, lambda p, at, table: coupled_extra(table, p, at[1], at[0])),
        ],
        out_specs=[pl.BlockSpec((2 * TB, TB), lambda p, at, table: (0, 0))] * 2,
        scratch_shapes=[pltpu.VMEM((TB, HB), jnp.float32)] * 3 + [pltpu.VMEM((TB, TB), jnp.float32)],
    )
    return pl.pallas_call(
        final_kernel,
        grid_spec=grid_spec,
        out_shape=[jax.ShapeDtypeStruct((2 * TB, TB), jnp.float32)] * 2,
        name="finish",
        cost_estimate=pl.CostEstimate(
            flops=25 * 6 * TB**3, bytes_accessed=64 * 2**20, transcendentals=0
        ),
        compiler_params=pltpu.CompilerParams(
            dimension_semantics=("arbitrary",), vmem_limit_bytes=60 * 2**20
        ),
    )(
        place, jnp.asarray(TABLE), solved, solved, vectors, vectors, vectors, lead, panel,
        gathered, extras, gathered, extras,
    )


def on_device(a_coupling, rhs, eig_vec, eig_val):
    row = lax.axis_index("row")
    col = lax.axis_index("col")
    half = col % 2
    tile_col = col // 2

    def trailing(stored):
        return jnp.concatenate([stored[HB:2 * HB, HB:], stored[3 * HB:, HB:]], axis=0)

    lead = plain(jnp.concatenate([a_coupling[:HB, HB:], a_coupling[2 * HB:3 * HB, HB:]], axis=0))
    vectors = eig_vec.reshape(NT, 2, 2, HB, TB)
    values = eig_val.reshape(NT, 2, 2, HB)[:, :, 1].reshape(NT, TB)

    def tile_vectors(index):
        return lax.dynamic_slice(
            vectors, (index, 0, 1, 0, 0), (1, 2, 1, HB, TB)
        ).reshape(TB, TB)

    coupled = tile_col < row
    left = mm(tile_vectors(row).T, jnp.where(coupled, trailing(a_coupling), trailing(rhs)))
    kept = lax.dynamic_slice_in_dim(left, half * HB, HB, 0)
    sent = lax.dynamic_slice_in_dim(left, (1 - half) * HB, HB, 0)
    other = lax.ppermute(sent, "col", [(i, i ^ 1) for i in range(16)])
    both = jnp.where(
        half == 0, jnp.concatenate([kept, other], axis=1), jnp.concatenate([other, kept], axis=1)
    )
    part = mm(both, tile_vectors(tile_col))
    turned = jnp.concatenate([part[:, :HB].T, part[:, HB:].T], axis=1)
    part = jnp.where(coupled, part, turned)
    def place(r, c):
        return r * 16 + c

    given = [
        lax.ppermute(
            part[MB:],
            ("row", "col"),
            [
                (place(i, 2 * j + h), place(home[0], 2 * home[1] + h))
                for (i, j), home in SPREAD.items() for h in range(2) if home[2] == slot
            ],
        )
        for slot in range(3)
    ]
    busy = coupled | (row + tile_col < NT)
    part = jnp.where(busy, part[:MB], jnp.concatenate(given, axis=0))
    gathered = lax.all_gather(part, ("row", "col"), axis=0, tiled=True)

    held, _ = lax.optimization_barrier((lead, part))
    pairs = [(r, c) for r in range(NT) for c in range(16)]
    straight = [(place(r, c), place(c // 2, 2 * r + c % 2)) for r, c in pairs]
    crossed = [(place(r, c), place(c // 2, 2 * r + 1 - c % 2)) for r, c in pairs]
    same = lax.ppermute(
        plain(lax.dynamic_slice_in_dim(held, half * HB, HB, 0)), ("row", "col"), straight
    )
    cross = lax.ppermute(
        plain(lax.dynamic_slice_in_dim(held, (1 - half) * HB, HB, 0)), ("row", "col"), crossed
    )
    block = plain(jnp.where(
        half == 0, jnp.concatenate([same, cross], axis=1), jnp.concatenate([cross, same], axis=1)
    ))
    val_row = values.reshape(NT, 1, TB)
    val_col = values.reshape(NT, TB, 1)
    lead, block, gathered, val_row, val_col = lax.optimization_barrier(
        (lead, block, gathered, val_row, val_col)
    )
    gathered = gathered.reshape(NT, NT, 2, MB, TB)

    lead_panel = lax.all_gather(plain(lead), "col", axis=0, tiled=True).reshape(NT, 2, TB, HB)
    col_panel = lax.all_gather(plain(block), "row", axis=0, tiled=True).reshape(NT, HB, TB)

    solved = solve(gathered, val_row, val_col)
    position = jnp.stack([row, tile_col, half]).astype(jnp.int32)
    return tuple(finish(position, solved, vectors, lead_panel, col_panel, gathered))


def solution(mesh):
    return jax.shard_map(
        on_device,
        mesh=mesh,
        in_specs=(P("row", "col"), P("row", "col"), P(), P()),
        out_specs=(P("row", "col"), P("row", "col")),
        check_vma=False,
    )
```

```python
import functools

import jax
import jax.numpy as jnp
import numpy as np
from jax import lax
from jax.experimental import pallas as pl
from jax.experimental.layout import Layout, with_layout_constraint
from jax.experimental.pallas import tpu as pltpu
from jax.sharding import PartitionSpec as P


TB = 512
HB = 256
NT = 8
QB = 64
MB = HB - QB


def spread_pairs():
    pairs = [(i, j) for i in range(NT) for j in range(NT)]
    idle = [(i, j) for i, j in pairs if i <= j and i + j >= NT]
    active = [pair for pair in pairs if pair not in idle]

    def ring(left, right):
        return min((left - right) % 4, (right - left) % 4)

    def distance(left, right):
        return (
            ring(left[0] // 2, right[0] // 2) + ring(left[1] // 2, right[1] // 2)
            + 2 * (left[1] % 2 != right[1] % 2)
        )

    found = {}
    for slot in range(3):
        for home in idle:
            near = min((p for p in active if p not in found), key=lambda p: distance(p, home))
            found[near] = (home[0], home[1], slot)
    return found


SPREAD = spread_pairs()
TABLE = np.array(
    [SPREAD.get((i, j), (0, 0, 0)) for i in range(NT) for j in range(NT)], np.int32
).reshape(-1)
EXTRA = (1, 1, 2, 1, QB, TB)


def extra_block(table, i, j):
    at = 3 * (NT * (i % NT) + j % NT)
    return (table[at], table[at + 1], 0, table[at + 2], 0, 0)


def mm(left_side, right_side, dims=None):
    if dims is None:
        dims = (((left_side.ndim - 1,), (0,)), ((), ()))
    return lax.dot_general(
        left_side, right_side, dims, precision=lax.Precision.HIGH, preferred_element_type=jnp.float32
    )


def plain(value):
    return with_layout_constraint(value, Layout((0, 1)))


def split(value):
    high = value.astype(jnp.bfloat16)
    low = (value - high.astype(jnp.float32)).astype(jnp.bfloat16)
    return high, low


def dot_nn(left, right):
    return lax.dot_general(left, right, (((1,), (0,)), ((), ())), preferred_element_type=jnp.float32)


def dot_nt(left, right):
    return lax.dot_general(left, right, (((1,), (1,)), ((), ())), preferred_element_type=jnp.float32)


def slot_of(p):
    return jnp.where(p >= 7, 25, jnp.where(p >= 6, 23, 4 * p))


def solve_kernel(
    rows_ref, cols_ref, table_ref, a_ref, a_extra_ref, r_ref, r_extra_0, r_extra_1, r_extra_2,
    r_extra_3, val_row_ref, out_ref, s_hi, s_lo, acc, t_hi, t_lo, stage, val_col, sems,
):
    step = pl.program_id(0)
    a = rows_ref[step]
    p = cols_ref[step]
    count = jnp.minimum(a, NT - a)

    def copies(n, a, b, i, j):
        return (
            pltpu.make_async_copy(
                stage.at[2 * n], out_ref.at[pl.ds(a * TB, TB), pl.ds(b * TB, TB)], sems.at[2 * n]
            ),
            pltpu.make_async_copy(
                stage.at[2 * n + 1], out_ref.at[pl.ds(i * TB, TB), pl.ds(j * TB, TB)],
                sems.at[2 * n + 1],
            ),
        )

    def drain(n):
        for copy in copies(n, 0, 0, 0, 0):
            copy.wait()

    for b, extra in enumerate((r_extra_0, r_extra_1, r_extra_2, r_extra_3)):
        @pl.when((p == 0) & ((b < count) | (b == a)))
        def _():
            for k in range(2):
                for h in range(2):
                    own = slice(k * HB, (k + 1) * HB)
                    across = slice(h * HB, (h + 1) * HB)
                    acc[b, k * HB:k * HB + MB, across] = r_ref[b, 0, h, :, own]
                    acc[b, k * HB + MB:(k + 1) * HB, across] = extra[0, 0, h, 0, :, own]

    def store(b, right_side, diagonal):
        down = jnp.concatenate([val_col[a]] * (TB // 128), axis=1)
        tile = -(right_side / (down + val_row_ref[b]))
        high, low = split(tile)
        s_hi[slot_of(a) + b] = high
        s_lo[slot_of(a) + b] = low
        n = b % 2
        stage[2 * n] = tile
        if diagonal:
            for copy in copies(n, a, b, NT - 1, NT - 1):
                copy.start()
        else:
            turned = tile.T
            stage[2 * n + 1] = turned

            @pl.when(a < 4)
            def _():
                high, low = split(turned)
                s_hi[4 * b + a] = high
                s_lo[4 * b + a] = low

            for copy in copies(n, a, b, b, a):
                copy.start()

    @pl.when(step == 0)
    def _():
        for i in range(NT):
            val_col[i] = jnp.broadcast_to(val_row_ref[i], (128, TB)).T
        stage[1] = jnp.zeros_like(stage[1])
        stage[3] = jnp.zeros_like(stage[3])
        store(0, acc[0], True)

    @pl.when(step > 0)
    def _():
        slot = jnp.where(a < 4, step - 1, 6)
        for k in range(2):
            high, low = split(a_ref[0, 0, k])
            t_hi[slot, k * HB:k * HB + MB] = high
            t_lo[slot, k * HB:k * HB + MB] = low
            high, low = split(a_extra_ref[0, 0, k, 0])
            t_hi[slot, k * HB + MB:(k + 1) * HB] = high
            t_lo[slot, k * HB + MB:(k + 1) * HB] = low

        def product(b, carry):
            s = slot_of(p) + b
            high, low = t_hi[slot], t_lo[slot]
            right_high, right_low = s_hi[s], s_lo[s]
            acc[b] -= dot_nn(high, right_high) + dot_nn(high, right_low) + dot_nn(low, right_high)
            return carry

        def two(b, carry):
            product(2 * b, carry)
            return product(2 * b + 1, carry)

        lax.fori_loop(0, count // 2, two, 0)

        @pl.when(count % 2 == 1)
        def _():
            product(count - 1, 0)

        def mirror(b, q, target):
            s = slot_of(a) + q
            t = b * (b - 1) // 2 + q
            high, low = s_hi[s], s_lo[s]
            right_high, right_low = t_hi[t], t_lo[t]
            acc[target] -= dot_nt(high, right_high) + dot_nt(high, right_low) + dot_nt(low, right_high)

        @pl.when(p == a - 1)
        def _():
            def tile(b, carry):
                def inner(q, carry):
                    mirror(b, q, b)
                    return carry

                lax.fori_loop(0, b, inner, 0)
                drain(b % 2)
                store(b, acc[b], False)
                return carry

            lax.fori_loop(0, count, tile, 0)

            @pl.when(a < 4)
            def _():
                acc[0] = jnp.zeros_like(acc[0])

                def inner(q, carry):
                    mirror(a, q, 0)
                    return carry

                lax.fori_loop(0, a, inner, 0)

                @pl.when(a > 1)
                def _():
                    drain(a % 2)

                store(a, acc[a] + acc[0] + acc[0].T, True)

    @pl.when(step == pl.num_programs(0) - 1)
    def _():
        drain(0)
        drain(1)


def solve(gathered, val_row):
    pairs = [(1, 0)] + [(a, p) for a in range(1, NT) for p in range(a)]
    extras = gathered.reshape(NT, NT, 2, 3, QB, TB)
    def at(t):
        return jnp.clip(t, 0, len(pairs) - 1)

    rows = np.array([0] + [a for a, _ in pairs[1:]] + [0] * 3, np.int32)
    cols = np.array([p for _, p in pairs] + [0] * 3, np.int32)
    grid_spec = pltpu.PrefetchScalarGridSpec(
        num_scalar_prefetch=3,
        grid=(len(pairs),),
        in_specs=[
            pl.BlockSpec(
                (1, 1, 2, MB, TB),
                lambda t, rows, cols, table: (jnp.maximum(rows[at(t)], 1), cols[at(t)], 0, 0, 0),
            ),
            pl.BlockSpec(
                EXTRA,
                lambda t, rows, cols, table: extra_block(
                    table, jnp.maximum(rows[at(t)], 1), cols[at(t)]
                ),
            ),
            pl.BlockSpec((4, 1, 2, MB, TB), lambda t, rows, cols, table: (0, rows[at(t)], 0, 0, 0)),
        ] + [
            pl.BlockSpec(
                EXTRA,
                functools.partial(
                    lambda b, t, rows, cols, table: extra_block(table, b, rows[at(t)]), b
                ),
            )
            for b in range(4)
        ] + [
            pl.BlockSpec((NT, 1, TB), lambda t, rows, cols, table: (0, 0, 0)),
        ],
        out_specs=pl.BlockSpec(memory_space=pl.ANY),
        scratch_shapes=[
            pltpu.VMEM((26, TB, TB), jnp.bfloat16),
            pltpu.VMEM((26, TB, TB), jnp.bfloat16),
            pltpu.VMEM((4, TB, TB), jnp.float32),
            pltpu.VMEM((7, TB, TB), jnp.bfloat16),
            pltpu.VMEM((7, TB, TB), jnp.bfloat16),
            pltpu.VMEM((4, TB, TB), jnp.float32),
            pltpu.VMEM((NT, TB, 128), jnp.float32),
            pltpu.SemaphoreType.DMA((4,)),
        ],
    )
    return pl.pallas_call(
        solve_kernel,
        grid_spec=grid_spec,
        out_shape=jax.ShapeDtypeStruct((NT * TB, NT * TB), jnp.float32),
        name="solve",
        cost_estimate=pl.CostEstimate(
            flops=84 * 6 * TB**3, bytes_accessed=90 * 2**20, transcendentals=0
        ),
        compiler_params=pltpu.CompilerParams(
            dimension_semantics=("arbitrary",), vmem_limit_bytes=63 * 2**20
        ),
    )(
        jnp.asarray(rows), jnp.asarray(cols), jnp.asarray(TABLE), gathered, extras, gathered,
        extras, extras, extras, extras, val_row,
    )


def dot3(left, right, dot):
    left_high, left_low = left
    right_high, right_low = right
    return dot(left_high, right_high) + (dot(left_high, right_low) + dot(left_low, right_high))


def final_kernel(
    place_ref, table_ref, s_col_ref, s_row_ref, v_p_ref, v_row_ref, v_half_ref, lead_ref, panel_ref,
    a_row_ref, a_row_extra_ref, a_col_ref, a_col_extra_ref, solution_ref, pending_ref, lead_sum, trail_sum, turn_sum, mirror_sum,
):
    p = pl.program_id(0)
    a = place_ref[0]
    b = place_ref[1]

    def whole(ref, i):
        return split(jnp.concatenate([ref[i(0)], ref[i(1)]], axis=0))

    def joined(ref, extra):
        parts = [ref[0, 0, 0], extra[0, 0, 0, 0], ref[0, 0, 1], extra[0, 0, 1, 0]]
        return split(jnp.concatenate(parts, axis=0))

    v_half = split(v_half_ref[0, 0, 0])

    @pl.when(p == 0)
    def _():
        for ref in (lead_sum, trail_sum, turn_sum, mirror_sum, solution_ref):
            ref[...] = jnp.zeros_like(ref)

    v_p = whole(v_p_ref, lambda k: (0, k, 0))
    s_col = split(jnp.where(p + b < NT, s_col_ref[...], 0.0))
    s_row = split(jnp.where(p + a < NT, s_row_ref[...], 0.0))
    turned = dot3(s_col, v_half, dot_nt)
    panel = dot3(split(panel_ref[0]), v_p, dot_nn)
    turned = split(turned)
    x = dot3(v_p, turned, dot_nn)
    turn_sum[...] += dot3(s_row, split(panel), dot_nt)
    lead = split(jnp.concatenate([lead_ref[0, 0], lead_ref[0, 1]], axis=1))
    lead_sum[...] += dot3(lead, split(x), dot_nn)

    @pl.when((p < a) & (p + b < NT))
    def _():
        trail_sum[...] += dot3(joined(a_row_ref, a_row_extra_ref), turned, dot_nn)

    @pl.when((p == a) & (p + b < NT))
    def _():
        solution_ref[HB:2 * HB, HB:] = x[:HB]
        solution_ref[3 * HB:, HB:] = x[HB:]

    @pl.when((p < b) & (p + a < NT))
    def _():
        mirror_sum[...] += dot3(s_row, joined(a_col_ref, a_col_extra_ref), dot_nt)

    @pl.when(p == NT - 1)
    def _():
        v_row = whole(v_row_ref, lambda k: (0, k, 0))
        trail = trail_sum[...] + dot3(split(mirror_sum[...]), v_half, dot_nt)
        turn = dot3(v_row, split(turn_sum[...]), dot_nn)
        trail = dot3(v_row, split(trail), dot_nn)
        for k in range(2):
            own = slice(k * HB, (k + 1) * HB)
            top = slice(2 * k * HB, (2 * k + 1) * HB)
            low = slice((2 * k + 1) * HB, (2 * k + 2) * HB)
            pending_ref[top, :HB] = jnp.zeros((HB, HB), jnp.float32)
            pending_ref[top, HB:] = lead_sum[own]
            pending_ref[low, :HB] = turn[own]
            pending_ref[low, HB:] = trail[own]


def finish(place, solved, vectors, lead, panel, gathered):
    tile = (1, 1, 2, MB, TB)
    least = jnp.minimum

    def coupled_block(p, own, across):
        return (own, least(p, jnp.maximum(least(own - 1, NT - 1 - across), 0)), 0, 0, 0)

    def coupled_extra(table, p, own, across):
        return extra_block(table, *coupled_block(p, own, across)[:2])

    extras = gathered.reshape(NT, NT, 2, 3, QB, TB)
    grid_spec = pltpu.PrefetchScalarGridSpec(
        num_scalar_prefetch=2,
        grid=(NT,),
        in_specs=[
            pl.BlockSpec((TB, TB), lambda p, at, table: (least(p, NT - 1 - at[1]), at[1])),
            pl.BlockSpec((TB, TB), lambda p, at, table: (at[0], least(p, NT - 1 - at[0]))),
            pl.BlockSpec((1, 2, 1, HB, TB), lambda p, at, table: (p, 0, 1, 0, 0)),
            pl.BlockSpec((1, 2, 1, HB, TB), lambda p, at, table: (at[0], 0, 1, 0, 0)),
            pl.BlockSpec((1, 1, 1, HB, TB), lambda p, at, table: (at[1], at[2], 1, 0, 0)),
            pl.BlockSpec((1, 2, TB, HB), lambda p, at, table: (least(p, NT - 1 - at[1]), 0, 0, 0)),
            pl.BlockSpec((1, HB, TB), lambda p, at, table: (least(p, NT - 1 - at[0]), 0, 0)),
            pl.BlockSpec(tile, lambda p, at, table: coupled_block(p, at[0], at[1])),
            pl.BlockSpec(EXTRA, lambda p, at, table: coupled_extra(table, p, at[0], at[1])),
            pl.BlockSpec(tile, lambda p, at, table: coupled_block(p, at[1], at[0])),
            pl.BlockSpec(EXTRA, lambda p, at, table: coupled_extra(table, p, at[1], at[0])),
        ],
        out_specs=[pl.BlockSpec((2 * TB, TB), lambda p, at, table: (0, 0))] * 2,
        scratch_shapes=[pltpu.VMEM((TB, HB), jnp.float32)] * 3 + [pltpu.VMEM((TB, TB), jnp.float32)],
    )
    return pl.pallas_call(
        final_kernel,
        grid_spec=grid_spec,
        out_shape=[jax.ShapeDtypeStruct((2 * TB, TB), jnp.float32)] * 2,
        name="finish",
        cost_estimate=pl.CostEstimate(
            flops=25 * 6 * TB**3, bytes_accessed=64 * 2**20, transcendentals=0
        ),
        compiler_params=pltpu.CompilerParams(
            dimension_semantics=("arbitrary",), vmem_limit_bytes=60 * 2**20
        ),
    )(
        place, jnp.asarray(TABLE), solved, solved, vectors, vectors, vectors, lead, panel,
        gathered, extras, gathered, extras,
    )


def on_device(a_coupling, rhs, eig_vec, eig_val):
    row = lax.axis_index("row")
    col = lax.axis_index("col")
    half = col % 2
    tile_col = col // 2

    def trailing(stored):
        return jnp.concatenate([stored[HB:2 * HB, HB:], stored[3 * HB:, HB:]], axis=0)

    lead = plain(jnp.concatenate([a_coupling[:HB, HB:], a_coupling[2 * HB:3 * HB, HB:]], axis=0))
    vectors = eig_vec.reshape(NT, 2, 2, HB, TB)
    values = eig_val.reshape(NT, 2, 2, HB)[:, :, 1].reshape(NT, TB)

    def tile_vectors(index):
        return lax.dynamic_slice(
            vectors, (index, 0, 1, 0, 0), (1, 2, 1, HB, TB)
        ).reshape(TB, TB)

    coupled = tile_col < row
    left = mm(tile_vectors(row).T, jnp.where(coupled, trailing(a_coupling), trailing(rhs)))
    kept = lax.dynamic_slice_in_dim(left, half * HB, HB, 0)
    sent = lax.dynamic_slice_in_dim(left, (1 - half) * HB, HB, 0)
    other = lax.ppermute(sent, "col", [(i, i ^ 1) for i in range(16)])
    both = jnp.where(
        half == 0, jnp.concatenate([kept, other], axis=1), jnp.concatenate([other, kept], axis=1)
    )
    part = mm(both, tile_vectors(tile_col))
    turned = jnp.concatenate([part[:, :HB].T, part[:, HB:].T], axis=1)
    part = jnp.where(coupled, part, turned)
    def place(r, c):
        return r * 16 + c

    given = [
        lax.ppermute(
            part[MB:],
            ("row", "col"),
            [
                (place(i, 2 * j + h), place(home[0], 2 * home[1] + h))
                for (i, j), home in SPREAD.items() for h in range(2) if home[2] == slot
            ],
        )
        for slot in range(3)
    ]
    busy = coupled | (row + tile_col < NT)
    part = jnp.where(busy, part[:MB], jnp.concatenate(given, axis=0))
    gathered = lax.all_gather(part, ("row", "col"), axis=0, tiled=True)

    held, _ = lax.optimization_barrier((lead, part))
    pairs = [(r, c) for r in range(NT) for c in range(16)]
    straight = [(place(r, c), place(c // 2, 2 * r + c % 2)) for r, c in pairs]
    crossed = [(place(r, c), place(c // 2, 2 * r + 1 - c % 2)) for r, c in pairs]
    same = lax.ppermute(
        plain(lax.dynamic_slice_in_dim(held, half * HB, HB, 0)), ("row", "col"), straight
    )
    cross = lax.ppermute(
        plain(lax.dynamic_slice_in_dim(held, (1 - half) * HB, HB, 0)), ("row", "col"), crossed
    )
    block = plain(jnp.where(
        half == 0, jnp.concatenate([same, cross], axis=1), jnp.concatenate([cross, same], axis=1)
    ))
    val_row = values.reshape(NT, 1, TB)
    lead, block, gathered = lax.optimization_barrier((lead, block, gathered))
    gathered = gathered.reshape(NT, NT, 2, MB, TB)

    lead_panel = lax.all_gather(plain(lead), "col", axis=0, tiled=True).reshape(NT, 2, TB, HB)
    col_panel = lax.all_gather(plain(block), "row", axis=0, tiled=True).reshape(NT, HB, TB)

    solved = solve(gathered, val_row)
    position = jnp.stack([row, tile_col, half]).astype(jnp.int32)
    return tuple(finish(position, solved, vectors, lead_panel, col_panel, gathered))


def solution(mesh):
    return jax.shard_map(
        on_device,
        mesh=mesh,
        in_specs=(P("row", "col"), P("row", "col"), P(), P()),
        out_specs=(P("row", "col"), P("row", "col")),
        check_vma=False,
    )
```
